128 devices in a mesh: outer: 8 (over x, core), inner: 16 (over y, z).
Axes of the slice: x: 4, y: 4, z: 4, core: 2. Of those that a mesh axis runs over, the one named last changes fastest.
Arguments:
- query: bfloat16 [524288, 256], P(('outer', 'inner')), may hold values from -6 to 6
- keys: bfloat16 [524288, 256], P(('outer', 'inner')), may hold values from -1.5 to 1.5
- values: bfloat16 [524288, 256], P(('outer', 'inner')), may hold values from -6 to 6
- out_grad: bfloat16 [524288, 256], P(('outer', 'inner')), may hold values from -1.5 to 1.5
Outputs:
- attended: bfloat16 [524288, 256], P(('outer', 'inner'))
- query_grad: bfloat16 [524288, 256], P(('outer', 'inner'))
- keys_grad: bfloat16 [524288, 256], P(('outer', 'inner'))
- values_grad: bfloat16 [524288, 256], P(('outer', 'inner'))
The draws below stay inside these ranges and needn't reach their ends.
All inputs are finite; a program needn't handle non-finite values.
Results may differ from the reference program's by a relative error of at most 0.008.
Values sent between devices are 32-bit elements; how exact they have to be, the bound alone decides.
A program may use at most 192 MiB of HBM per device.

```python
import jax
import jax.numpy as jnp
from jax import lax

H = 2
E = 128
BLK = 512
TOKENS = 524288


def steps_of(own_key, extent, shards, low, top_value):
    factor_of = 1.0
    for dim, blocks in shards:
        steps = jax.random.uniform(jax.random.fold_in(jax.random.fold_in(own_key, 6), dim), (blocks,), jnp.float32, low / len(shards), top_value / len(shards))
        factor_of = factor_of * jnp.repeat(jnp.exp(steps), extent[dim] // blocks).reshape((-1,) + (1,) * (len(extent) - 1 - dim))
    return factor_of


def centred(rng, extent, scale, reach, pieces=(), kind=jnp.bfloat16):
    values = jax.random.normal(rng, extent, jnp.float32) * scale
    if len(pieces) > 0:
        values = steps_of(rng, extent, pieces, -0.22, 0.18) * values
    return jnp.clip(values, min=-reach, max=reach).astype(kind)


def setup_inputs(seed: int = 0) -> dict:
    splits = jax.random.split(jax.random.key(seed), 5)
    return {
        "query": centred(splits[0], (TOKENS, H * E), 1.0, 6.0, ((0, 128),)),
        "keys": centred(splits[1], (TOKENS, H * E), 0.25, 1.5, ((0, 128),)),
        "values": centred(splits[2], (TOKENS, H * E), 1.0, 6.0, ((0, 128),)),
        "out_grad": centred(splits[3], (TOKENS, H * E), 0.25, 1.5, ((0, 128),)),
    }


def block_terms(query_block, keys_block, values_block, grad_block, scaling):
    scaled = (query_block.astype(jnp.float32) * scaling[:, None, None]).astype(jnp.bfloat16)
    causal = jnp.tril(jnp.ones((BLK, BLK), dtype=bool))[None]
    ascore = jnp.einsum('thd,shd->hts', scaled.astype(jnp.float32), keys_block.astype(jnp.float32))
    bscore = jnp.einsum('the,she->hts', grad_block.astype(jnp.float32), values_block.astype(jnp.float32))
    amat = jnp.where(causal, ascore, 0.0).astype(jnp.bfloat16)
    bmat = jnp.where(causal, bscore, 0.0).astype(jnp.bfloat16)
    return scaled, amat, bmat


def reference(query, keys, values, out_grad):
    blocks = TOKENS // BLK

    def split(array):
        return array.reshape(blocks, BLK, H, E)

    position = jnp.arange(TOKENS, dtype=jnp.int32).reshape(blocks, BLK)
    scaling = (position.astype(jnp.float32) + 1.0) ** -0.5
    inputs = (split(query), split(keys), split(values), split(out_grad), scaling)
    highest = lax.Precision.HIGHEST

    def forward_step(state, items):
        query_block, keys_block, values_block, grad_block, scale_row = items
        scaled, amat, bmat = block_terms(query_block, keys_block, values_block, grad_block, scale_row)
        attended = jnp.einsum('hts,she->the', amat.astype(jnp.float32), values_block.astype(jnp.float32))
        attended = attended + jnp.einsum('thd,hde->the', scaled.astype(jnp.float32), state, precision=highest)
        qgrad = jnp.einsum('hts,shd->thd', bmat.astype(jnp.float32), keys_block.astype(jnp.float32))
        qgrad = qgrad + jnp.einsum('the,hde->thd', grad_block.astype(jnp.float32), state, precision=highest)
        qgrad = qgrad * scale_row[:, None, None]
        state = state + jnp.einsum('shd,she->hde', keys_block.astype(jnp.float32), values_block.astype(jnp.float32))
        return state, (attended.astype(jnp.bfloat16), qgrad.astype(jnp.bfloat16))

    def backward_step(state, items):
        query_block, keys_block, values_block, grad_block, scale_row = items
        scaled, amat, bmat = block_terms(query_block, keys_block, values_block, grad_block, scale_row)
        kgrad = jnp.einsum('hts,thd->shd', bmat.astype(jnp.float32), scaled.astype(jnp.float32))
        kgrad = kgrad + jnp.einsum('she,hde->shd', values_block.astype(jnp.float32), state, precision=highest)
        vgrad = jnp.einsum('hts,the->she', amat.astype(jnp.float32), grad_block.astype(jnp.float32))
        vgrad = vgrad + jnp.einsum('shd,hde->she', keys_block.astype(jnp.float32), state, precision=highest)
        state = state + jnp.einsum('thd,the->hde', scaled.astype(jnp.float32), grad_block.astype(jnp.float32))
        return state, (kgrad.astype(jnp.bfloat16), vgrad.astype(jnp.bfloat16))

    start = jnp.zeros((H, E, E), jnp.float32)
    last, (attended, qgrad) = lax.scan(forward_step, start, inputs)
    first, (kgrad, vgrad) = lax.scan(backward_step, start, inputs, reverse=True)
    width = H * E
    return (attended.reshape(TOKENS, width), qgrad.reshape(TOKENS, width),
            kgrad.reshape(TOKENS, width), vgrad.reshape(TOKENS, width))
```

```python
import functools

import jax
import jax.numpy as jnp
from jax import lax
from jax.experimental import pallas as pl
from jax.experimental.pallas import tpu as pltpu
from jax.sharding import PartitionSpec as P

H = 2
E = 128
TILE = 256
CHUNK = 512
STEP = 1024
MESH = pl.DeviceIdType.MESH
F32 = jnp.float32
BF16 = jnp.bfloat16
NN = (((1,), (0,)), ((), ()))
NT = (((1,), (1,)), ((), ()))
TN = (((0,), (0,)), ((), ()))


def dot(a, b, dims):
    return lax.dot_general(a, b, dims, preferred_element_type=F32)


def coefficient(first, rows):
    place = lax.broadcasted_iota(jnp.int32, (rows, E), 0) + first
    return lax.rsqrt(place.astype(F32) + 1.0)


def states_kernel(
    n_outer, n_inner,
    query, keys, values, grad,
    kv_states, qg_states,
    q_in, k_in, v_in, g_in, kv_local, qg_local,
    mine, arrived, done, total, totals, finished,
    in_sem, send_a, recv_a, send_b, recv_b, send_c, recv_c,
):
    outer = lax.axis_index("outer")
    inner = lax.axis_index("inner")
    rows = query.shape[0]
    chunks = rows // CHUNK
    per_chunk = CHUNK // TILE
    part = E * H // n_inner

    def load(which, source, target, chunk):
        span = pl.ds(pl.multiple_of(chunk * CHUNK, CHUNK), CHUNK)
        return pltpu.make_async_copy(source.at[span], target.at[span], in_sem.at[which, chunk])

    @pl.loop(0, chunks)
    def _(chunk):
        load(0, keys, k_in, chunk).start()
        load(1, values, v_in, chunk).start()
        load(2, query, q_in, chunks - 1 - chunk).start()
        load(3, grad, g_in, chunks - 1 - chunk).start()

    barrier = pltpu.get_barrier_semaphore()

    @pl.loop(1, n_inner)
    def _(step):
        peer = lax.rem(inner + step, n_inner)
        pl.semaphore_signal(barrier, inc=1, device_id=(outer, peer), device_id_type=MESH)

    @pl.loop(1, n_outer)
    def _(step):
        peer = lax.rem(outer + step, n_outer)
        pl.semaphore_signal(barrier, inc=1, device_id=(peer, inner), device_id_type=MESH)

    first = (outer * n_inner + inner) * rows

    def accumulate(chunk, sums):
        kv, qg = list(sums[:H]), list(sums[H:])
        load(0, keys, k_in, chunk).wait()
        load(1, values, v_in, chunk).wait()
        for b in range(per_chunk):
            block = chunk * per_chunk + b
            span = pl.ds(pl.multiple_of(block * TILE, TILE), TILE)
            for h in range(H):
                cols = slice(h * E, (h + 1) * E)
                kv_local[block, h] = kv[h]
                kv[h] = kv[h] + dot(k_in[span, cols], v_in[span, cols], TN)
        back = chunks - 1 - chunk
        load(2, query, q_in, back).wait()
        load(3, grad, g_in, back).wait()
        for b in range(per_chunk - 1, -1, -1):
            block = back * per_chunk + b
            span = pl.ds(pl.multiple_of(block * TILE, TILE), TILE)
            scale = coefficient(first + block * TILE, TILE)
            for h in range(H):
                cols = slice(h * E, (h + 1) * E)
                qg_local[block, h] = qg[h]
                scaled = (q_in[span, cols].astype(F32) * scale).astype(BF16)
                qg[h] = qg[h] + dot(scaled, g_in[span, cols], TN)
        return tuple(kv) + tuple(qg)

    zero = jnp.zeros((E, E), F32)
    sums = lax.fori_loop(0, chunks, accumulate, (zero,) * (2 * H))
    for h in range(H):
        share = n_inner // H
        mine[h * share:(h + 1) * share, 0:part] = sums[h].reshape(share, part, E)
        mine[h * share:(h + 1) * share, part:2 * part] = sums[H + h].reshape(share, part, E)

    pl.semaphore_wait(barrier, n_inner + n_outer - 2)

    def hand_out(step):
        peer = lax.rem(inner + step, n_inner)
        return pltpu.make_async_remote_copy(
            src_ref=mine.at[peer], dst_ref=arrived.at[inner],
            send_sem=send_a.at[peer], recv_sem=recv_a.at[inner],
            device_id=(outer, peer), device_id_type=MESH)

    def take_in(step):
        peer = lax.rem(inner + step, n_inner)
        return pltpu.make_async_remote_copy(
            src_ref=mine.at[peer], dst_ref=arrived.at[peer],
            send_sem=send_a.at[peer], recv_sem=recv_a.at[peer],
            device_id=(outer, peer), device_id_type=MESH)

    @pl.loop(1, n_inner)
    def _(step):
        hand_out(step).start()

    arrived[inner] = mine[inner]

    @pl.loop(1, n_inner)
    def _(step):
        take_in(step).wait_recv()

    kv = jnp.zeros((part, E), F32)
    qg = jnp.zeros((part, E), F32)
    for j in range(n_inner):
        done[j, 0:part] = kv
        kv = kv + arrived[j, 0:part]
        k = n_inner - 1 - j
        done[k, part:2 * part] = qg
        qg = qg + arrived[k, part:2 * part]
    total[0:part] = kv
    total[part:2 * part] = qg

    def spread(step):
        peer = lax.rem(outer + step, n_outer)
        return pltpu.make_async_remote_copy(
            src_ref=total, dst_ref=totals.at[outer],
            send_sem=send_b.at[peer], recv_sem=recv_b.at[outer],
            device_id=(peer, inner), device_id_type=MESH)

    def collect(step):
        peer = lax.rem(outer + step, n_outer)
        return pltpu.make_async_remote_copy(
            src_ref=total, dst_ref=totals.at[peer],
            send_sem=send_b.at[peer], recv_sem=recv_b.at[peer],
            device_id=(peer, inner), device_id_type=MESH)

    @pl.loop(1, n_outer)
    def _(step):
        spread(step).start()

    totals[outer] = total[...]

    @pl.loop(1, n_outer)
    def _(step):
        collect(step).wait_recv()

    kv = jnp.zeros((part, E), F32)
    qg = jnp.zeros((part, E), F32)
    for j in range(n_outer):
        kv = kv + jnp.where(j < outer, totals[j, 0:part], 0.0)
        qg = qg + jnp.where(j > outer, totals[j, part:2 * part], 0.0)
    for j in range(n_inner):
        done[j, 0:part] = done[j, 0:part] + kv
        done[j, part:2 * part] = done[j, part:2 * part] + qg

    def hand_back(step):
        peer = lax.rem(inner + step, n_inner)
        return pltpu.make_async_remote_copy(
            src_ref=done.at[peer], dst_ref=finished.at[inner],
            send_sem=send_c.at[peer], recv_sem=recv_c.at[inner],
            device_id=(outer, peer), device_id_type=MESH)

    def take_back(step):
        peer = lax.rem(inner + step, n_inner)
        return pltpu.make_async_remote_copy(
            src_ref=done.at[peer], dst_ref=finished.at[peer],
            send_sem=send_c.at[peer], recv_sem=recv_c.at[peer],
            device_id=(outer, peer), device_id_type=MESH)

    @pl.loop(1, n_inner)
    def _(step):
        hand_back(step).start()

    finished[inner] = done[inner]

    @pl.loop(1, n_inner)
    def _(step):
        take_back(step).wait_recv()

    share = n_inner // H
    for h in range(H):
        span = slice(h * share, (h + 1) * share)
        kv = finished[span, 0:part].reshape(E, E)
        qg = finished[span, part:2 * part].reshape(E, E)

        @pl.loop(0, rows // TILE)
        def _(block):
            kv_states[block, h] = (kv_local[block, h] + kv).astype(BF16)
            qg_states[block, h] = (qg_local[block, h] + qg).astype(BF16)

    @pl.loop(1, n_inner)
    def _(step):
        hand_out(step).wait_send()
        hand_back(step).wait_send()

    @pl.loop(1, n_outer)
    def _(step):
        spread(step).wait_send()


def outputs_kernel(n_inner, total_rows, query, keys, values, grad, kv_states, qg_states, attended, qgrad, kgrad, vgrad):
    outer = lax.axis_index("outer")
    inner = lax.axis_index("inner")
    first = (outer * n_inner + inner) * total_rows + pl.program_id(0) * STEP
    row = lax.broadcasted_iota(jnp.int32, (TILE, TILE), 0)
    col = lax.broadcasted_iota(jnp.int32, (TILE, TILE), 1)
    causal = row >= col
    zero = jnp.zeros((E, E), BF16)

    def both(state):
        top = jnp.concatenate([state[0], zero], axis=1)
        bottom = jnp.concatenate([zero, state[1]], axis=1)
        return jnp.concatenate([top, bottom], axis=0)

    for b in range(STEP // TILE):
        span = slice(b * TILE, (b + 1) * TILE)
        scale = coefficient(first + b * TILE, TILE)
        wide = jnp.concatenate([scale] * H, axis=1)
        scaled = (query[span].astype(F32) * wide).astype(BF16)
        k, v, g = keys[span], values[span], grad[span]
        kv, qg = both(kv_states[b]), both(qg_states[b])
        state_parts = (dot(scaled, kv, NN), dot(g, kv, NT), dot(v, qg, NT), dot(k, qg, NN))
        for h in range(H):
            cols = slice(h * E, (h + 1) * E)
            a = jnp.where(causal, dot(scaled[:, cols], k[:, cols], NT), 0.0).astype(BF16)
            d = jnp.where(causal, dot(g[:, cols], v[:, cols], NT), 0.0).astype(BF16)
            attended[span, cols] = (dot(a, v[:, cols], NN) + state_parts[0][:, cols]).astype(BF16)
            qgrad[span, cols] = ((dot(d, k[:, cols], NN) + state_parts[1][:, cols]) * scale).astype(BF16)
            kgrad[span, cols] = (dot(d, scaled[:, cols], TN) + state_parts[2][:, cols]).astype(BF16)
            vgrad[span, cols] = (dot(a, g[:, cols], TN) + state_parts[3][:, cols]).astype(BF16)


def on_device(n_outer, n_inner, query, keys, values, out_grad):
    rows, width = query.shape
    blocks = rows // TILE
    part = E * H // n_inner
    anywhere = pl.BlockSpec(memory_space=pl.ANY)
    in_vmem = pl.BlockSpec(memory_space=pltpu.VMEM)
    slices = pltpu.VMEM((n_inner, 2 * part, E), F32)
    dma = pltpu.SemaphoreType.DMA
    states = jax.ShapeDtypeStruct((blocks, H, E, E), BF16)
    kv_states, qg_states = pl.pallas_call(
        functools.partial(states_kernel, n_outer, n_inner),
        out_shape=(states, states),
        in_specs=[anywhere] * 4,
        out_specs=(in_vmem, in_vmem),
        scratch_shapes=[pltpu.VMEM((rows, width), BF16)] * 4
        + [pltpu.VMEM((blocks, H, E, E), F32)] * 2
        + [slices, slices, slices, pltpu.VMEM((2 * part, E), F32),
           pltpu.VMEM((n_outer, 2 * part, E), F32), slices]
        + [dma((4, rows // CHUNK)), dma((n_inner,)), dma((n_inner,)), dma((n_outer,)),
           dma((n_outer,)), dma((n_inner,)), dma((n_inner,))],
        compiler_params=pltpu.CompilerParams(
            collective_id=0, has_side_effects=True, vmem_limit_bytes=32 << 20),
        name="states",
    )(query, keys, values, out_grad)
    data = pl.BlockSpec((STEP, width), lambda i: (i, 0))
    state = pl.BlockSpec((STEP // TILE, H, E, E), lambda i: (i, 0, 0, 0))
    result = jax.ShapeDtypeStruct((rows, width), BF16)
    return pl.pallas_call(
        functools.partial(outputs_kernel, n_inner, rows),
        grid=(rows // STEP,),
        out_shape=(result,) * 4,
        in_specs=[data] * 4 + [state] * 2,
        out_specs=(data,) * 4,
        compiler_params=pltpu.CompilerParams(vmem_limit_bytes=32 << 20),
        name="outputs",
    )(query, keys, values, out_grad, kv_states, qg_states)


def solution(mesh):
    spec = P(("outer", "inner"), None)
    return jax.shard_map(
        functools.partial(on_device, mesh.shape["outer"], mesh.shape["inner"]),
        mesh=mesh,
        in_specs=(spec,) * 4,
        out_specs=(spec,) * 4,
        check_vma=False,
    )
```

```python
import functools

import jax
import jax.numpy as jnp
from jax import lax
from jax.experimental import pallas as pl
from jax.experimental.pallas import tpu as pltpu
from jax.sharding import PartitionSpec as P

H = 2
E = 128
TILE = 256
CHUNK = 512
OUT = 512
SPLIT = (3, 6, 8)
MESH = pl.DeviceIdType.MESH
F32 = jnp.float32
BF16 = jnp.bfloat16
NN = (((1,), (0,)), ((), ()))
NT = (((1,), (1,)), ((), ()))
TN = (((0,), (0,)), ((), ()))


def dot(a, b, dims):
    return lax.dot_general(a, b, dims, preferred_element_type=F32)


def coefficient(first, rows):
    place = lax.broadcasted_iota(jnp.int32, (rows, E), 0) + first
    return lax.rsqrt(place.astype(F32) + 1.0)


def both_heads(first, second):
    zero = jnp.zeros((E, E), BF16)
    top = jnp.concatenate([first, zero], axis=1)
    bottom = jnp.concatenate([zero, second], axis=1)
    return jnp.concatenate([top, bottom], axis=0)


def local_kernel(
    n_outer, n_inner,
    query, keys, values, grad,
    scaled, k_in, v_in, g_in, att_sum, qgrad_sum, kgrad_sum, vgrad_sum, before,
    kv_local, qg_local, mine, arrived, done, total, totals, finished,
    in_sem, send_a, recv_a, send_b, recv_b, send_c, recv_c,
):
    outer = lax.axis_index("outer")
    inner = lax.axis_index("inner")
    rows = query.shape[0]
    chunks = rows // CHUNK
    per_chunk = CHUNK // TILE
    part = E * H // n_inner

    def load(which, source, target, chunk):
        span = pl.ds(pl.multiple_of(chunk * CHUNK, CHUNK), CHUNK)
        return pltpu.make_async_copy(source.at[span], target.at[span], in_sem.at[which, chunk])

    @pl.loop(0, chunks)
    def _(chunk):
        load(0, keys, k_in, chunk).start()
        load(1, values, v_in, chunk).start()
        load(2, query, scaled, chunks - 1 - chunk).start()
        load(3, grad, g_in, chunks - 1 - chunk).start()

    barrier = pltpu.get_barrier_semaphore()

    @pl.loop(1, n_inner)
    def _(step):
        peer = lax.rem(inner + step, n_inner)
        pl.semaphore_signal(barrier, inc=1, device_id=(outer, peer), device_id_type=MESH)

    @pl.loop(1, n_outer)
    def _(step):
        peer = lax.rem(outer + step, n_outer)
        pl.semaphore_signal(barrier, inc=1, device_id=(peer, inner), device_id_type=MESH)

    first = (outer * n_inner + inner) * rows

    def accumulate(chunk, sums):
        kv, qg = list(sums[:H]), list(sums[H:])
        load(0, keys, k_in, chunk).wait()
        load(1, values, v_in, chunk).wait()
        for b in range(per_chunk):
            block = chunk * per_chunk + b
            span = pl.ds(pl.multiple_of(block * TILE, TILE), TILE)
            for h in range(H):
                cols = slice(h * E, (h + 1) * E)
                kv_local[block, h] = kv[h].astype(BF16)
                kv[h] = kv[h] + dot(k_in[span, cols], v_in[span, cols], TN)
        back = chunks - 1 - chunk
        load(2, query, scaled, back).wait()
        load(3, grad, g_in, back).wait()
        for b in range(per_chunk - 1, -1, -1):
            block = back * per_chunk + b
            span = pl.ds(pl.multiple_of(block * TILE, TILE), TILE)
            scale = coefficient(first + block * TILE, TILE)
            for h in range(H):
                cols = slice(h * E, (h + 1) * E)
                qg_local[block, h] = qg[h].astype(BF16)
                qs = (scaled[span, cols].astype(F32) * scale).astype(BF16)
                scaled[span, cols] = qs
                qg[h] = qg[h] + dot(qs, g_in[span, cols], TN)
        return tuple(kv) + tuple(qg)

    zero = jnp.zeros((E, E), F32)
    sums = lax.fori_loop(0, chunks, accumulate, (zero,) * (2 * H))
    share = n_inner // H
    for h in range(H):
        mine[h * share:(h + 1) * share, 0:part] = sums[h].reshape(share, part, E)
        mine[h * share:(h + 1) * share, part:2 * part] = sums[H + h].reshape(share, part, E)

    row = lax.broadcasted_iota(jnp.int32, (TILE, TILE), 0)
    col = lax.broadcasted_iota(jnp.int32, (TILE, TILE), 1)
    causal = row >= col

    def local_terms(start, stop):
        @pl.loop(start, stop)
        def _(pair):
            for b in range(2):
                block = pair * 2 + b
                span = pl.ds(pl.multiple_of(block * TILE, TILE), TILE)
                qs, k, v, g = scaled[span], k_in[span], v_in[span], g_in[span]
                kv = both_heads(kv_local[block, 0], kv_local[block, 1])
                qg = both_heads(qg_local[block, 0], qg_local[block, 1])
                state_parts = (dot(qs, kv, NN), dot(g, kv, NT), dot(v, qg, NT), dot(k, qg, NN))
                for h in range(H):
                    cols = slice(h * E, (h + 1) * E)
                    a = jnp.where(causal, dot(qs[:, cols], k[:, cols], NT), 0.0).astype(BF16)
                    d = jnp.where(causal, dot(g[:, cols], v[:, cols], NT), 0.0).astype(BF16)
                    att_sum[span, cols] = dot(a, v[:, cols], NN) + state_parts[0][:, cols]
                    qgrad_sum[span, cols] = dot(d, k[:, cols], NN) + state_parts[1][:, cols]
                    kgrad_sum[span, cols] = dot(d, qs[:, cols], TN) + state_parts[2][:, cols]
                    vgrad_sum[span, cols] = dot(a, g[:, cols], TN) + state_parts[3][:, cols]

    pl.semaphore_wait(barrier, n_inner + n_outer - 2)

    def over_inner(source, target, send, recv, step, slot):
        peer = lax.rem(inner + step, n_inner)
        slot = inner if slot is None else peer
        return pltpu.make_async_remote_copy(
            src_ref=source.at[peer], dst_ref=target.at[slot],
            send_sem=send.at[peer], recv_sem=recv.at[slot],
            device_id=(outer, peer), device_id_type=MESH)

    def over_outer(step, slot):
        peer = lax.rem(outer + step, n_outer)
        slot = outer if slot is None else peer
        return pltpu.make_async_remote_copy(
            src_ref=total, dst_ref=totals.at[slot],
            send_sem=send_b.at[peer], recv_sem=recv_b.at[slot],
            device_id=(peer, inner), device_id_type=MESH)

    @pl.loop(1, n_inner)
    def _(step):
        over_inner(mine, arrived, send_a, recv_a, step, None).start()

    arrived[inner] = mine[inner]
    local_terms(0, SPLIT[0])

    @pl.loop(1, n_inner)
    def _(step):
        over_inner(mine, arrived, send_a, recv_a, step, 1).wait_recv()

    kv = jnp.zeros((part, E), F32)
    qg = jnp.zeros((part, E), F32)
    for j in range(n_inner):
        done[j, 0:part] = kv
        kv = kv + arrived[j, 0:part]
        k = n_inner - 1 - j
        done[k, part:2 * part] = qg
        qg = qg + arrived[k, part:2 * part]
    total[0:part] = kv
    total[part:2 * part] = qg

    @pl.loop(1, n_outer)
    def _(step):
        over_outer(step, None).start()

    totals[outer] = total[...]
    local_terms(SPLIT[0], SPLIT[1])

    @pl.loop(1, n_outer)
    def _(step):
        over_outer(step, 1).wait_recv()

    kv = jnp.zeros((part, E), F32)
    qg = jnp.zeros((part, E), F32)
    for j in range(n_outer):
        kv = kv + jnp.where(j < outer, totals[j, 0:part], 0.0)
        qg = qg + jnp.where(j > outer, totals[j, part:2 * part], 0.0)
    for j in range(n_inner):
        done[j, 0:part] = done[j, 0:part] + kv
        done[j, part:2 * part] = done[j, part:2 * part] + qg

    @pl.loop(1, n_inner)
    def _(step):
        over_inner(done, finished, send_c, recv_c, step, None).start()

    finished[inner] = done[inner]
    local_terms(SPLIT[1], SPLIT[2])

    @pl.loop(1, n_inner)
    def _(step):
        over_inner(done, finished, send_c, recv_c, step, 1).wait_recv()

    for h in range(H):
        span = slice(h * share, (h + 1) * share)
        before[0, h] = finished[span, 0:part].reshape(E, E).astype(BF16)
        before[1, h] = finished[span, part:2 * part].reshape(E, E).astype(BF16)

    @pl.loop(1, n_inner)
    def _(step):
        over_inner(mine, arrived, send_a, recv_a, step, None).wait_send()
        over_inner(done, finished, send_c, recv_c, step, None).wait_send()

    @pl.loop(1, n_outer)
    def _(step):
        over_outer(step, None).wait_send()


def finish_kernel(
    n_inner, scaled, k_in, v_in, g_in, att_sum, qgrad_sum, kgrad_sum, vgrad_sum, before,
    attended, qgrad, kgrad, vgrad, att_out, qgrad_out, kgrad_out, vgrad_out, sem,
):
    rows = scaled.shape[0]
    first = (lax.axis_index("outer") * n_inner + lax.axis_index("inner")) * rows
    kv = both_heads(before[0, 0], before[0, 1])
    qg = both_heads(before[1, 0], before[1, 1])

    def store(which, source, target, tile):
        span = pl.ds(pl.multiple_of(tile * OUT, OUT), OUT)
        return pltpu.make_async_copy(source.at[span], target.at[span], sem.at[which, tile])

    stores = ((att_out, attended), (qgrad_out, qgrad), (kgrad_out, kgrad), (vgrad_out, vgrad))

    @pl.loop(0, rows // OUT)
    def _(tile):
        span = pl.ds(pl.multiple_of(tile * OUT, OUT), OUT)
        scale = coefficient(first + tile * OUT, OUT)
        wide = jnp.concatenate([scale] * H, axis=1)
        att_out[span] = (att_sum[span] + dot(scaled[span], kv, NN)).astype(BF16)
        qgrad_out[span] = ((qgrad_sum[span] + dot(g_in[span], kv, NT)) * wide).astype(BF16)
        kgrad_out[span] = (kgrad_sum[span] + dot(v_in[span], qg, NT)).astype(BF16)
        vgrad_out[span] = (vgrad_sum[span] + dot(k_in[span], qg, NN)).astype(BF16)
        for which, (source, target) in enumerate(stores):
            store(which, source, target, tile).start()

    @pl.loop(0, rows // OUT)
    def _(tile):
        for which, (source, target) in enumerate(stores):
            store(which, source, target, tile).wait()


def on_device(n_outer, n_inner, query, keys, values, out_grad):
    rows, width = query.shape
    blocks = rows // TILE
    part = E * H // n_inner
    anywhere = pl.BlockSpec(memory_space=pl.ANY)
    in_vmem = pl.BlockSpec(memory_space=pltpu.VMEM)
    slices = pltpu.VMEM((n_inner, 2 * part, E), F32)
    dma = pltpu.SemaphoreType.DMA
    data = jax.ShapeDtypeStruct((rows, width), BF16)
    sums = jax.ShapeDtypeStruct((rows, width), F32)
    local = pl.pallas_call(
        functools.partial(local_kernel, n_outer, n_inner),
        out_shape=(data,) * 4 + (sums,) * 4 + (jax.ShapeDtypeStruct((2, H, E, E), BF16),),
        in_specs=[anywhere] * 4,
        out_specs=(in_vmem,) * 9,
        scratch_shapes=[pltpu.VMEM((blocks, H, E, E), BF16)] * 2
        + [slices, slices, slices, pltpu.VMEM((2 * part, E), F32),
           pltpu.VMEM((n_outer, 2 * part, E), F32), slices]
        + [dma((4, rows // CHUNK)), dma((n_inner,)), dma((n_inner,)), dma((n_outer,)),
           dma((n_outer,)), dma((n_inner,)), dma((n_inner,))],
        compiler_params=pltpu.CompilerParams(
            collective_id=0, has_side_effects=True, vmem_limit_bytes=12 << 20),
        name="local",
    )(*[pltpu.with_memory_space_constraint(x, pltpu.HBM) for x in (query, keys, values, out_grad)])
    return pl.pallas_call(
        functools.partial(finish_kernel, n_inner),
        out_shape=(data,) * 4,
        in_specs=[in_vmem] * 9,
        out_specs=(anywhere,) * 4,
        scratch_shapes=[pltpu.VMEM((rows, width), BF16)] * 4 + [dma((4, rows // OUT))],
        compiler_params=pltpu.CompilerParams(vmem_limit_bytes=16 << 20),
        name="finish",
    )(*local)


def solution(mesh):
    spec = P(("outer", "inner"), None)
    return jax.shard_map(
        functools.partial(on_device, mesh.shape["outer"], mesh.shape["inner"]),
        mesh=mesh,
        in_specs=(spec,) * 4,
        out_specs=(spec,) * 4,
        check_vma=False,
    )
```

```python
import functools

import jax
import jax.numpy as jnp
from jax import lax
from jax.experimental import pallas as pl
from jax.experimental.pallas import tpu as pltpu
from jax.sharding import PartitionSpec as P

H = 2
E = 128
TILE = 256
CHUNK = 2048
OUT = 1024
GROUP = 4
SPLIT = (2, 3, 4)
MESH = pl.DeviceIdType.MESH
F32 = jnp.float32
BF16 = jnp.bfloat16
NN = (((1,), (0,)), ((), ()))
NT = (((1,), (1,)), ((), ()))
TN = (((0,), (0,)), ((), ()))


def dot(a, b, dims):
    return lax.dot_general(a, b, dims, preferred_element_type=F32)


def coefficient(first, rows):
    place = lax.broadcasted_iota(jnp.int32, (rows, E), 0) + first
    return lax.rsqrt(place.astype(F32) + 1.0)


def both_heads(first, second):
    zero = jnp.zeros((E, E), BF16)
    top = jnp.concatenate([first, zero], axis=1)
    bottom = jnp.concatenate([zero, second], axis=1)
    return jnp.concatenate([top, bottom], axis=0)


def local_kernel(
    n_outer, n_inner,
    query, keys, values, grad,
    scaled, k_in, v_in, g_in, att_sum, qgrad_sum, kgrad_sum, vgrad_sum, before,
    kv_local, qg_local, totals_of, mine, arrived, done, total, totals, finished,
    in_sem, send_a, recv_a, send_b, recv_b, send_c, recv_c,
):
    outer = lax.axis_index("outer")
    inner = lax.axis_index("inner")
    rows = query.shape[0]
    chunks = rows // CHUNK
    per_chunk = CHUNK // TILE
    part = E * H // n_inner

    def load(which, source, target, chunk):
        span = pl.ds(pl.multiple_of(chunk * CHUNK, CHUNK), CHUNK)
        return pltpu.make_async_copy(source.at[span], target.at[span], in_sem.at[which, chunk])

    for chunk in range(chunks):
        load(0, keys, k_in, chunk).start()
        load(1, values, v_in, chunk).start()
    for chunk in reversed(range(chunks)):
        load(2, query, scaled, chunk).start()
        load(3, grad, g_in, chunk).start()

    barrier = pltpu.get_barrier_semaphore()

    @pl.loop(1, n_inner)
    def _(step):
        peer = lax.rem(inner + step, n_inner)
        pl.semaphore_signal(barrier, inc=1, device_id=(outer, peer), device_id_type=MESH)

    @pl.loop(1, n_outer)
    def _(step):
        peer = lax.rem(outer + step, n_outer)
        pl.semaphore_signal(barrier, inc=1, device_id=(peer, inner), device_id_type=MESH)

    first = (outer * n_inner + inner) * rows

    totals_of[...] = jnp.zeros_like(totals_of)

    @pl.loop(0, chunks)
    def _(chunk):
        load(0, keys, k_in, chunk).wait()
        load(1, values, v_in, chunk).wait()
        for h in range(H):
            cols = slice(h * E, (h + 1) * E)
            kv = totals_of[0, h]
            for b in range(per_chunk):
                block = chunk * per_chunk + b
                span = pl.ds(pl.multiple_of(block * TILE, TILE), TILE)
                kv_local[block, h] = kv.astype(BF16)
                kv = kv + dot(k_in[span, cols], v_in[span, cols], TN)
            totals_of[0, h] = kv

    @pl.loop(0, chunks)
    def _(turn):
        chunk = chunks - 1 - turn
        load(2, query, scaled, chunk).wait()
        load(3, grad, g_in, chunk).wait()
        for h in range(H):
            cols = slice(h * E, (h + 1) * E)
            qg = totals_of[1, h]
            for b in reversed(range(per_chunk)):
                block = chunk * per_chunk + b
                span = pl.ds(pl.multiple_of(block * TILE, TILE), TILE)
                scale = coefficient(first + block * TILE, TILE)
                qg_local[block, h] = qg.astype(BF16)
                qs = (scaled[span, cols].astype(F32) * scale).astype(BF16)
                scaled[span, cols] = qs
                qg = qg + dot(qs, g_in[span, cols], TN)
            totals_of[1, h] = qg

    share = n_inner // H
    for h in range(H):
        for s in range(2):
            mine[h * share:(h + 1) * share, s * part:(s + 1) * part] = totals_of[s, h].reshape(share, part, E)

    row = lax.broadcasted_iota(jnp.int32, (TILE, TILE), 0)
    col = lax.broadcasted_iota(jnp.int32, (TILE, TILE), 1)
    causal = row >= col

    def local_terms(start, stop):
        @pl.loop(start, stop)
        def _(group):
            for b in range(GROUP):
                block = group * GROUP + b
                span = pl.ds(pl.multiple_of(block * TILE, TILE), TILE)
                for h in range(H):
                    cols = slice(h * E, (h + 1) * E)
                    qs, k, v, g = scaled[span, cols], k_in[span, cols], v_in[span, cols], g_in[span, cols]
                    kv, qg = kv_local[block, h], qg_local[block, h]
                    a = jnp.where(causal, dot(qs, k, NT), 0.0).astype(BF16)
                    d = jnp.where(causal, dot(g, v, NT), 0.0).astype(BF16)
                    att_sum[span, cols] = dot(
                        jnp.concatenate([a, qs], axis=1), jnp.concatenate([v, kv], axis=0), NN)
                    qgrad_sum[span, cols] = dot(
                        jnp.concatenate([d, g], axis=1), jnp.concatenate([k, kv.T], axis=0), NN)
                    kgrad_sum[span, cols] = dot(d, qs, TN) + dot(v, qg, NT)
                    vgrad_sum[span, cols] = dot(a, g, TN) + dot(k, qg, NN)

    pl.semaphore_wait(barrier, n_inner + n_outer - 2)

    side = 4
    plane = [(a, b) for a in range(n_inner // side) for b in range(side) if (a, b) != (0, 0)]
    plane.sort(key=lambda o: -min(o[0], n_inner // side - o[0]) - min(o[1], side - o[1]))
    line = [(a, b) for a in range(n_outer // 2) for b in range(2) if (a, b) != (0, 0)]
    line.sort(key=lambda o: -3 * min(o[0], n_outer // 2 - o[0]) - o[1])

    def shifted(place, offset, width, sizes, sign):
        high = lax.rem(place // width + sizes + sign * offset[0], sizes)
        low = lax.rem(lax.rem(place, width) + width + sign * offset[1], width)
        return high * width + low

    def over_inner(source, target, send, recv, offset, landing=False):
        peer = shifted(inner, offset, side, n_inner // side, 1)
        slot = shifted(inner, offset, side, n_inner // side, -1) if landing else inner
        return pltpu.make_async_remote_copy(
            src_ref=source.at[peer], dst_ref=target.at[slot],
            send_sem=send.at[peer], recv_sem=recv.at[slot],
            device_id=(outer, peer), device_id_type=MESH)

    def over_outer(offset, landing=False):
        peer = shifted(outer, offset, 2, n_outer // 2, 1)
        slot = shifted(outer, offset, 2, n_outer // 2, -1) if landing else outer
        return pltpu.make_async_remote_copy(
            src_ref=total, dst_ref=totals.at[slot],
            send_sem=send_b.at[peer], recv_sem=recv_b.at[slot],
            device_id=(peer, inner), device_id_type=MESH)

    for offset in plane:
        over_inner(mine, arrived, send_a, recv_a, offset).start()

    arrived[inner] = mine[inner]
    local_terms(0, SPLIT[0])

    for offset in reversed(plane):
        over_inner(mine, arrived, send_a, recv_a, offset, True).wait_recv()

    kv = jnp.zeros((part, E), F32)
    qg = jnp.zeros((part, E), F32)
    for j in range(n_inner):
        done[j, 0:part] = kv
        kv = kv + arrived[j, 0:part]
        k = n_inner - 1 - j
        done[k, part:2 * part] = qg
        qg = qg + arrived[k, part:2 * part]
    total[0:part] = kv
    total[part:2 * part] = qg

    for offset in line:
        over_outer(offset).start()

    totals[outer] = total[...]
    local_terms(SPLIT[0], SPLIT[1])

    for offset in reversed(line):
        over_outer(offset, True).wait_recv()

    kv = jnp.zeros((part, E), F32)
    qg = jnp.zeros((part, E), F32)
    for j in range(n_outer):
        kv = kv + jnp.where(j < outer, totals[j, 0:part], 0.0)
        qg = qg + jnp.where(j > outer, totals[j, part:2 * part], 0.0)
    for j in range(n_inner):
        done[j, 0:part] = done[j, 0:part] + kv
        done[j, part:2 * part] = done[j, part:2 * part] + qg

    for offset in plane:
        over_inner(done, finished, send_c, recv_c, offset).start()

    finished[inner] = done[inner]
    local_terms(SPLIT[1], SPLIT[2])

    for offset in reversed(plane):
        over_inner(done, finished, send_c, recv_c, offset, True).wait_recv()

    for h in range(H):
        span = slice(h * share, (h + 1) * share)
        before[0, h] = finished[span, 0:part].reshape(E, E).astype(BF16)
        before[1, h] = finished[span, part:2 * part].reshape(E, E).astype(BF16)

    for offset in plane:
        over_inner(mine, arrived, send_a, recv_a, offset).wait_send()
        over_inner(done, finished, send_c, recv_c, offset).wait_send()
    for offset in line:
        over_outer(offset).wait_send()


def finish_kernel(
    n_inner, scaled, k_in, v_in, g_in, att_sum, qgrad_sum, kgrad_sum, vgrad_sum, before,
    attended, qgrad, kgrad, vgrad, att_out, qgrad_out, kgrad_out, vgrad_out, sem,
):
    rows = scaled.shape[0]
    first = (lax.axis_index("outer") * n_inner + lax.axis_index("inner")) * rows
    kv = both_heads(before[0, 0], before[0, 1])
    qg = both_heads(before[1, 0], before[1, 1])

    def store(which, source, target, tile):
        span = pl.ds(pl.multiple_of(tile * OUT, OUT), OUT)
        return pltpu.make_async_copy(source.at[span], target.at[span], sem.at[which, tile])

    stores = ((att_out, attended), (qgrad_out, qgrad), (kgrad_out, kgrad), (vgrad_out, vgrad))

    @pl.loop(0, rows // OUT)
    def _(tile):
        span = pl.ds(pl.multiple_of(tile * OUT, OUT), OUT)
        scale = coefficient(first + tile * OUT, OUT)
        wide = jnp.concatenate([scale] * H, axis=1)
        att_out[span] = (att_sum[span] + dot(scaled[span], kv, NN)).astype(BF16)
        qgrad_out[span] = ((qgrad_sum[span] + dot(g_in[span], kv, NT)) * wide).astype(BF16)
        kgrad_out[span] = (kgrad_sum[span] + dot(v_in[span], qg, NT)).astype(BF16)
        vgrad_out[span] = (vgrad_sum[span] + dot(k_in[span], qg, NN)).astype(BF16)
        for which, (source, target) in enumerate(stores):
            store(which, source, target, tile).start()

    @pl.loop(0, rows // OUT)
    def _(tile):
        for which, (source, target) in enumerate(stores):
            store(which, source, target, tile).wait()


def on_device(n_outer, n_inner, query, keys, values, out_grad):
    rows, width = query.shape
    blocks = rows // TILE
    part = E * H // n_inner
    anywhere = pl.BlockSpec(memory_space=pl.ANY)
    in_vmem = pl.BlockSpec(memory_space=pltpu.VMEM)
    slices = pltpu.VMEM((n_inner, 2 * part, E), F32)
    dma = pltpu.SemaphoreType.DMA
    data = jax.ShapeDtypeStruct((rows, width), BF16)
    sums = jax.ShapeDtypeStruct((rows, width), F32)
    local = pl.pallas_call(
        functools.partial(local_kernel, n_outer, n_inner),
        out_shape=(data,) * 4 + (sums,) * 4 + (jax.ShapeDtypeStruct((2, H, E, E), BF16),),
        in_specs=[anywhere] * 4,
        out_specs=(in_vmem,) * 9,
        scratch_shapes=[pltpu.VMEM((blocks, H, E, E), BF16)] * 2
        + [pltpu.VMEM((2, H, E, E), F32), slices, slices, slices, pltpu.VMEM((2 * part, E), F32),
           pltpu.VMEM((n_outer, 2 * part, E), F32), slices]
        + [dma((4, rows // CHUNK)), dma((n_inner,)), dma((n_inner,)), dma((n_outer,)),
           dma((n_outer,)), dma((n_inner,)), dma((n_inner,))],
        compiler_params=pltpu.CompilerParams(
            collective_id=0, has_side_effects=True, vmem_limit_bytes=12 << 20),
        name="local",
    )(*[pltpu.with_memory_space_constraint(x, pltpu.HBM) for x in (query, keys, values, out_grad)])
    return pl.pallas_call(
        functools.partial(finish_kernel, n_inner),
        out_shape=(data,) * 4,
        in_specs=[in_vmem] * 9,
        out_specs=(anywhere,) * 4,
        scratch_shapes=[pltpu.VMEM((rows, width), BF16)] * 4 + [dma((4, rows // OUT))],
        compiler_params=pltpu.CompilerParams(vmem_limit_bytes=16 << 20),
        name="finish",
    )(*local)


def solution(mesh):
    spec = P(("outer", "inner"), None)
    return jax.shard_map(
        functools.partial(on_device, mesh.shape["outer"], mesh.shape["inner"]),
        mesh=mesh,
        in_specs=(spec,) * 4,
        out_specs=(spec,) * 4,
        check_vma=False,
    )
```

```python
import functools

import jax
import jax.numpy as jnp
from jax import lax
from jax.experimental import pallas as pl
from jax.experimental.pallas import tpu as pltpu
from jax.sharding import PartitionSpec as P

H = 2
E = 128
TILE = 256
CHUNK = 2048
SIZES = (512,) * 8
SPLIT = (6, 12, 16)
MESH = pl.DeviceIdType.MESH
F32 = jnp.float32
BF16 = jnp.bfloat16
NN = (((1,), (0,)), ((), ()))
NT = (((1,), (1,)), ((), ()))
TN = (((0,), (0,)), ((), ()))


def dot(a, b, dims):
    return lax.dot_general(a, b, dims, preferred_element_type=F32)


def coefficient(first, rows):
    place = lax.broadcasted_iota(jnp.int32, (rows, E), 0) + first
    return lax.rsqrt(place.astype(F32) + 1.0)


def both_heads(first, second):
    zero = jnp.zeros((E, E), BF16)
    top = jnp.concatenate([first, zero], axis=1)
    bottom = jnp.concatenate([zero, second], axis=1)
    return jnp.concatenate([top, bottom], axis=0)


def local_kernel(
    n_outer, n_inner,
    query, keys, values, grad,
    scaled, k_in, v_in, g_in, att_sum, qgrad_sum, kgrad_sum, vgrad_sum, before,
    kv_local, qg_local, totals_of, mine, arrived, done, total, totals, finished,
    in_sem, send_a, recv_a, send_b, recv_b, send_c, recv_c,
):
    outer = lax.axis_index("outer")
    inner = lax.axis_index("inner")
    rows = query.shape[0]
    chunks = rows // CHUNK
    per_chunk = CHUNK // TILE
    part = E * H // n_inner

    def load(which, source, target, chunk):
        span = pl.ds(pl.multiple_of(chunk * CHUNK, CHUNK), CHUNK)
        return pltpu.make_async_copy(source.at[span], target.at[span], in_sem.at[which, chunk])

    for chunk in range(chunks):
        load(0, keys, k_in, chunk).start()
        load(1, values, v_in, chunk).start()
    for chunk in reversed(range(chunks)):
        load(2, query, scaled, chunk).start()
        load(3, grad, g_in, chunk).start()

    totals[...] = jnp.zeros_like(totals)
    barrier = pltpu.get_barrier_semaphore()

    @pl.loop(1, n_inner)
    def _(step):
        peer = lax.rem(inner + step, n_inner)
        pl.semaphore_signal(barrier, inc=1, device_id=(outer, peer), device_id_type=MESH)

    @pl.loop(1, n_outer)
    def _(step):
        peer = lax.rem(outer + step, n_outer)
        pl.semaphore_signal(barrier, inc=1, device_id=(peer, inner), device_id_type=MESH)

    first = (outer * n_inner + inner) * rows

    totals_of[...] = jnp.zeros_like(totals_of)

    @pl.loop(0, chunks)
    def _(chunk):
        load(0, keys, k_in, chunk).wait()
        load(1, values, v_in, chunk).wait()
        for h in range(H):
            cols = slice(h * E, (h + 1) * E)
            kv = totals_of[0, h]
            for b in range(per_chunk):
                block = chunk * per_chunk + b
                span = pl.ds(pl.multiple_of(block * TILE, TILE), TILE)
                kv_local[block, h] = kv.astype(BF16)
                kv = kv + dot(k_in[span, cols], v_in[span, cols], TN)
            totals_of[0, h] = kv

    @pl.loop(0, chunks)
    def _(turn):
        chunk = chunks - 1 - turn
        load(2, query, scaled, chunk).wait()
        load(3, grad, g_in, chunk).wait()
        for h in range(H):
            cols = slice(h * E, (h + 1) * E)
            qg = totals_of[1, h]
            for b in reversed(range(per_chunk)):
                block = chunk * per_chunk + b
                span = pl.ds(pl.multiple_of(block * TILE, TILE), TILE)
                scale = coefficient(first + block * TILE, TILE)
                qg_local[block, h] = qg.astype(BF16)
                qs = (scaled[span, cols].astype(F32) * scale).astype(BF16)
                scaled[span, cols] = qs
                qg = qg + dot(qs, g_in[span, cols], TN)
            totals_of[1, h] = qg

    share = n_inner // H
    for h in range(H):
        for s in range(2):
            mine[h * share:(h + 1) * share, s * part:(s + 1) * part] = totals_of[s, h].reshape(share, part, E)

    row = lax.broadcasted_iota(jnp.int32, (TILE, TILE), 0)
    col = lax.broadcasted_iota(jnp.int32, (TILE, TILE), 1)
    causal = row >= col

    def local_terms(start, stop):
        for block in range(start, stop):
            span = pl.ds(block * TILE, TILE)
            for h in range(H):
                cols = slice(h * E, (h + 1) * E)
                qs, k, v, g = scaled[span, cols], k_in[span, cols], v_in[span, cols], g_in[span, cols]
                kv, qg = kv_local[block, h], qg_local[block, h]
                a = jnp.where(causal, dot(qs, k, NT), 0.0).astype(BF16)
                d = jnp.where(causal, dot(g, v, NT), 0.0).astype(BF16)
                att_sum[span, cols] = dot(
                    jnp.concatenate([a, qs], axis=1), jnp.concatenate([v, kv], axis=0), NN)
                qgrad_sum[span, cols] = dot(
                    jnp.concatenate([d, g], axis=1), jnp.concatenate([k, kv.T], axis=0), NN)
                kgrad_sum[span, cols] = dot(d, qs, TN) + dot(v, qg, NT)
                vgrad_sum[span, cols] = dot(a, g, TN) + dot(k, qg, NN)

    pl.semaphore_wait(barrier, n_inner + n_outer - 2)

    side = 4
    plane = [(a, b) for a in range(n_inner // side) for b in range(side) if (a, b) != (0, 0)]
    plane.sort(key=lambda o: -min(o[0], n_inner // side - o[0]) - min(o[1], side - o[1]))
    line = [(a, b) for a in range(n_outer // 2) for b in range(2) if (a, b) != (0, 0)]
    line.sort(key=lambda o: -3 * min(o[0], n_outer // 2 - o[0]) - o[1])

    def shifted(place, offset, width, sizes, sign):
        high = lax.rem(place // width + sizes + sign * offset[0], sizes)
        low = lax.rem(lax.rem(place, width) + width + sign * offset[1], width)
        return high * width + low

    def over_inner(source, target, send, recv, offset, landing=False):
        peer = shifted(inner, offset, side, n_inner // side, 1)
        slot = shifted(inner, offset, side, n_inner // side, -1) if landing else inner
        return pltpu.make_async_remote_copy(
            src_ref=source.at[peer], dst_ref=target.at[slot],
            send_sem=send.at[peer], recv_sem=recv.at[slot],
            device_id=(outer, peer), device_id_type=MESH)

    def over_outer(offset, landing=False):
        peer = shifted(outer, offset, 2, n_outer // 2, 1)
        slot = shifted(outer, offset, 2, n_outer // 2, -1) if landing else outer
        goal = outer if landing else peer
        half = 1 - (goal + n_outer - slot) // n_outer
        span = pl.ds(pl.multiple_of(half * part, part), part)
        return pltpu.make_async_remote_copy(
            src_ref=total.at[span], dst_ref=totals.at[slot, span],
            send_sem=send_b.at[peer], recv_sem=recv_b.at[slot],
            device_id=(peer, inner), device_id_type=MESH)

    for offset in plane:
        over_inner(mine, arrived, send_a, recv_a, offset).start()

    arrived[inner] = mine[inner]
    local_terms(0, SPLIT[0])

    for offset in reversed(plane):
        over_inner(mine, arrived, send_a, recv_a, offset, True).wait_recv()

    kv = arrived[0, 0:part]
    qg = arrived[0, part:2 * part]
    for j in range(1, n_inner):
        kv = kv + arrived[j, 0:part]
        qg = qg + arrived[j, part:2 * part]
    total[0:part] = kv
    total[part:2 * part] = qg

    for offset in line:
        over_outer(offset).start()

    kv = jnp.zeros((part, E), F32)
    qg = jnp.zeros((part, E), F32)
    for j in range(n_inner):
        done[j, 0:part] = kv
        kv = kv + arrived[j, 0:part]
        k = n_inner - 1 - j
        done[k, part:2 * part] = qg
        qg = qg + arrived[k, part:2 * part]

    local_terms(SPLIT[0], SPLIT[1])

    for offset in reversed(line):
        over_outer(offset, True).wait_recv()

    kv = jnp.zeros((part, E), F32)
    qg = jnp.zeros((part, E), F32)
    for j in range(n_outer):
        kv = kv + totals[j, 0:part]
        qg = qg + totals[j, part:2 * part]
    for j in range(n_inner):
        done[j, 0:part] = done[j, 0:part] + kv
        done[j, part:2 * part] = done[j, part:2 * part] + qg

    for offset in plane:
        over_inner(done, finished, send_c, recv_c, offset).start()

    finished[inner] = done[inner]
    local_terms(SPLIT[1], SPLIT[2])

    for offset in reversed(plane):
        over_inner(done, finished, send_c, recv_c, offset, True).wait_recv()

    for h in range(H):
        span = slice(h * share, (h + 1) * share)
        before[0, h] = finished[span, 0:part].reshape(E, E).astype(BF16)
        before[1, h] = finished[span, part:2 * part].reshape(E, E).astype(BF16)

    for offset in plane:
        over_inner(mine, arrived, send_a, recv_a, offset).wait_send()
        over_inner(done, finished, send_c, recv_c, offset).wait_send()
    for offset in line:
        over_outer(offset).wait_send()


def finish_kernel(
    n_inner, scaled, k_in, v_in, g_in, att_sum, qgrad_sum, kgrad_sum, vgrad_sum, before,
    attended, qgrad, kgrad, vgrad, att_out, qgrad_out, kgrad_out, vgrad_out, sem,
):
    rows = scaled.shape[0]
    first = (lax.axis_index("outer") * n_inner + lax.axis_index("inner")) * rows
    kv = both_heads(before[0, 0], before[0, 1])
    qg = both_heads(before[1, 0], before[1, 1])

    tiles = []
    start = 0
    for size in SIZES:
        tiles.append((start, size))
        start += size

    def store(which, source, target, tile):
        span = pl.ds(*tiles[tile])
        return pltpu.make_async_copy(source.at[span], target.at[span], sem.at[which, tile])

    stores = ((att_out, attended), (qgrad_out, qgrad), (kgrad_out, kgrad), (vgrad_out, vgrad))
    for tile, (start, size) in enumerate(tiles):
        span = pl.ds(start, size)
        att_out[span] = (att_sum[span] + dot(scaled[span], kv, NN)).astype(BF16)
        store(0, *stores[0], tile).start()
        kgrad_out[span] = (kgrad_sum[span] + dot(v_in[span], qg, NT)).astype(BF16)
        store(2, *stores[2], tile).start()
        vgrad_out[span] = (vgrad_sum[span] + dot(k_in[span], qg, NN)).astype(BF16)
        store(3, *stores[3], tile).start()
        wide = jnp.concatenate([coefficient(first + start, size)] * H, axis=1)
        qgrad_out[span] = ((qgrad_sum[span] + dot(g_in[span], kv, NT)) * wide).astype(BF16)
        store(1, *stores[1], tile).start()
    for tile in range(len(tiles)):
        for which, pair in enumerate(stores):
            store(which, *pair, tile).wait()


def on_device(n_outer, n_inner, query, keys, values, out_grad):
    rows, width = query.shape
    blocks = rows // TILE
    part = E * H // n_inner
    anywhere = pl.BlockSpec(memory_space=pl.ANY)
    in_vmem = pl.BlockSpec(memory_space=pltpu.VMEM)
    slices = pltpu.VMEM((n_inner, 2 * part, E), F32)
    dma = pltpu.SemaphoreType.DMA
    data = jax.ShapeDtypeStruct((rows, width), BF16)
    sums = jax.ShapeDtypeStruct((rows, width), F32)
    local = pl.pallas_call(
        functools.partial(local_kernel, n_outer, n_inner),
        out_shape=(data,) * 4 + (sums,) * 4 + (jax.ShapeDtypeStruct((2, H, E, E), BF16),),
        in_specs=[anywhere] * 4,
        out_specs=(in_vmem,) * 9,
        scratch_shapes=[pltpu.VMEM((blocks, H, E, E), BF16)] * 2
        + [pltpu.VMEM((2, H, E, E), F32), slices, slices, slices, pltpu.VMEM((2 * part, E), F32),
           pltpu.VMEM((n_outer, 2 * part, E), F32), slices]
        + [dma((4, rows // CHUNK)), dma((n_inner,)), dma((n_inner,)), dma((n_outer,)),
           dma((n_outer,)), dma((n_inner,)), dma((n_inner,))],
        compiler_params=pltpu.CompilerParams(
            collective_id=0, has_side_effects=True, vmem_limit_bytes=12 << 20),
        name="local",
    )(*[pltpu.with_memory_space_constraint(x, pltpu.HBM) for x in (query, keys, values, out_grad)])
    return pl.pallas_call(
        functools.partial(finish_kernel, n_inner),
        out_shape=(data,) * 4,
        in_specs=[in_vmem] * 9,
        out_specs=(anywhere,) * 4,
        scratch_shapes=[pltpu.VMEM((rows, width), BF16)] * 4 + [dma((4, len(SIZES)))],
        compiler_params=pltpu.CompilerParams(vmem_limit_bytes=16 << 20),
        name="finish",
    )(*local)


def solution(mesh):
    spec = P(("outer", "inner"), None)
    return jax.shard_map(
        functools.partial(on_device, mesh.shape["outer"], mesh.shape["inner"]),
        mesh=mesh,
        in_specs=(spec,) * 4,
        out_specs=(spec,) * 4,
        check_vma=False,
    )
```

```python
import functools

import jax
import jax.numpy as jnp
from jax import lax
from jax.experimental import pallas as pl
from jax.experimental.pallas import tpu as pltpu
from jax.sharding import PartitionSpec as P

H = 2
E = 128
TILE = 256
CHUNK = 2048
SIZES = (512,) * 8
SPLIT = (7, 13, 16)
MESH = pl.DeviceIdType.MESH
F32 = jnp.float32
BF16 = jnp.bfloat16
NN = (((1,), (0,)), ((), ()))
NT = (((1,), (1,)), ((), ()))
TN = (((0,), (0,)), ((), ()))


def dot(a, b, dims):
    return lax.dot_general(a, b, dims, preferred_element_type=F32)


def coefficient(first, rows):
    place = lax.broadcasted_iota(jnp.int32, (rows, E), 0) + first
    return lax.rsqrt(place.astype(F32) + 1.0)


def both_heads(first, second):
    zero = jnp.zeros((E, E), BF16)
    top = jnp.concatenate([first, zero], axis=1)
    bottom = jnp.concatenate([zero, second], axis=1)
    return jnp.concatenate([top, bottom], axis=0)


def local_kernel(
    n_outer, n_inner,
    query, keys, values, grad,
    scaled, k_in, v_in, g_in, att_sum, qgrad_sum, kgrad_sum, vgrad_sum, before,
    kv_local, qg_local, totals_of, mine, arrived, done, total, totals, finished,
    in_sem, send_a, recv_a, send_b, recv_b, send_c, recv_c,
):
    outer = lax.axis_index("outer")
    inner = lax.axis_index("inner")
    rows = query.shape[0]
    chunks = rows // CHUNK
    per_chunk = CHUNK // TILE
    part = E * H // n_inner

    def load(which, source, target, chunk):
        span = pl.ds(pl.multiple_of(chunk * CHUNK, CHUNK), CHUNK)
        return pltpu.make_async_copy(source.at[span], target.at[span], in_sem.at[which, chunk])

    for chunk in range(chunks):
        load(0, keys, k_in, chunk).start()
        load(1, values, v_in, chunk).start()
    for chunk in reversed(range(chunks)):
        load(2, query, scaled, chunk).start()
        load(3, grad, g_in, chunk).start()

    side = 4
    plane = [(a, b) for a in range(n_inner // side) for b in range(side) if (a, b) != (0, 0)]
    plane.sort(key=lambda o: -min(o[0], n_inner // side - o[0]) - min(o[1], side - o[1]))
    line = [(a, b) for a in range(n_outer // 2) for b in range(2) if (a, b) != (0, 0)]
    line.sort(key=lambda o: -3 * min(o[0], n_outer // 2 - o[0]) - o[1])

    def shifted(place, offset, width, sizes):
        high = lax.rem(place // width + offset[0], sizes)
        low = lax.rem(lax.rem(place, width) + offset[1], width)
        return high * width + low

    there = {o: shifted(inner, o, side, n_inner // side) for o in plane}
    across = {o: shifted(outer, o, 2, n_outer // 2) for o in line}

    def back(offset, high, low):
        return (high - offset[0]) % high, (low - offset[1]) % low

    totals[...] = jnp.zeros_like(totals)
    barrier = pltpu.get_barrier_semaphore()

    for peer in there.values():
        pl.semaphore_signal(barrier, inc=1, device_id=(outer, peer), device_id_type=MESH)
    for peer in across.values():
        pl.semaphore_signal(barrier, inc=1, device_id=(peer, inner), device_id_type=MESH)

    first = (outer * n_inner + inner) * rows

    totals_of[...] = jnp.zeros_like(totals_of)

    @pl.loop(0, chunks)
    def _(chunk):
        load(0, keys, k_in, chunk).wait()
        load(1, values, v_in, chunk).wait()
        for h in range(H):
            cols = slice(h * E, (h + 1) * E)
            kv = totals_of[0, h]
            for b in range(per_chunk):
                block = chunk * per_chunk + b
                span = pl.ds(pl.multiple_of(block * TILE, TILE), TILE)
                kv_local[block, h] = kv.astype(BF16)
                kv = kv + dot(k_in[span, cols], v_in[span, cols], TN)
            totals_of[0, h] = kv

    @pl.loop(0, chunks)
    def _(turn):
        chunk = chunks - 1 - turn
        load(2, query, scaled, chunk).wait()
        load(3, grad, g_in, chunk).wait()
        for h in range(H):
            cols = slice(h * E, (h + 1) * E)
            qg = totals_of[1, h]
            for b in reversed(range(per_chunk)):
                block = chunk * per_chunk + b
                span = pl.ds(pl.multiple_of(block * TILE, TILE), TILE)
                scale = coefficient(first + block * TILE, TILE)
                qg_local[block, h] = qg.astype(BF16)
                qs = (scaled[span, cols].astype(F32) * scale).astype(BF16)
                scaled[span, cols] = qs
                qg = qg + dot(qs, g_in[span, cols], TN)
            totals_of[1, h] = qg

    share = n_inner // H
    for h in range(H):
        for s in range(2):
            mine[h * share:(h + 1) * share, s * part:(s + 1) * part] = totals_of[s, h].reshape(share, part, E)

    row = lax.broadcasted_iota(jnp.int32, (TILE, TILE), 0)
    col = lax.broadcasted_iota(jnp.int32, (TILE, TILE), 1)
    causal = row >= col

    def local_terms(start, stop):
        for block in range(start, stop):
            span = pl.ds(block * TILE, TILE)
            for h in range(H):
                cols = slice(h * E, (h + 1) * E)
                qs, k, v, g = scaled[span, cols], k_in[span, cols], v_in[span, cols], g_in[span, cols]
                kv, qg = kv_local[block, h], qg_local[block, h]
                a = jnp.where(causal, dot(qs, k, NT), 0.0).astype(BF16)
                d = jnp.where(causal, dot(g, v, NT), 0.0).astype(BF16)
                att_sum[span, cols] = dot(
                    jnp.concatenate([a, qs], axis=1), jnp.concatenate([v, kv], axis=0), NN)
                qgrad_sum[span, cols] = dot(
                    jnp.concatenate([d, g], axis=1), jnp.concatenate([k, kv.T], axis=0), NN)
                kgrad_sum[span, cols] = dot(d, qs, TN) + dot(v, qg, NT)
                vgrad_sum[span, cols] = dot(a, g, TN) + dot(k, qg, NN)

    pl.semaphore_wait(barrier, n_inner + n_outer - 2)

    def over_inner(source, target, send, recv, offset, landing=False):
        peer = there[offset]
        slot = there[back(offset, n_inner // side, side)] if landing else inner
        return pltpu.make_async_remote_copy(
            src_ref=source.at[peer], dst_ref=target.at[slot],
            send_sem=send.at[peer], recv_sem=recv.at[slot],
            device_id=(outer, peer), device_id_type=MESH)

    def over_outer(offset, landing=False):
        peer = across[offset]
        slot = across[back(offset, n_outer // 2, 2)] if landing else outer
        goal = outer if landing else peer
        half = 1 - (goal + n_outer - slot) // n_outer
        span = pl.ds(pl.multiple_of(half * part, part), part)
        return pltpu.make_async_remote_copy(
            src_ref=total.at[span], dst_ref=totals.at[slot, span],
            send_sem=send_b.at[peer], recv_sem=recv_b.at[slot],
            device_id=(peer, inner), device_id_type=MESH)

    for offset in plane:
        over_inner(mine, arrived, send_a, recv_a, offset).start()

    arrived[inner] = mine[inner]
    local_terms(0, SPLIT[0])

    for offset in reversed(plane):
        over_inner(mine, arrived, send_a, recv_a, offset, True).wait_recv()

    kv = arrived[0, 0:part]
    qg = arrived[0, part:2 * part]
    for j in range(1, n_inner):
        kv = kv + arrived[j, 0:part]
        qg = qg + arrived[j, part:2 * part]
    total[0:part] = kv
    total[part:2 * part] = qg

    for offset in line:
        over_outer(offset).start()

    kv = jnp.zeros((part, E), F32)
    qg = jnp.zeros((part, E), F32)
    for j in range(n_inner):
        done[j, 0:part] = kv
        kv = kv + arrived[j, 0:part]
        k = n_inner - 1 - j
        done[k, part:2 * part] = qg
        qg = qg + arrived[k, part:2 * part]

    local_terms(SPLIT[0], SPLIT[1])

    for offset in reversed(line):
        over_outer(offset, True).wait_recv()

    kv = jnp.zeros((part, E), F32)
    qg = jnp.zeros((part, E), F32)
    for j in range(n_outer):
        kv = kv + totals[j, 0:part]
        qg = qg + totals[j, part:2 * part]
    for j in range(n_inner):
        done[j, 0:part] = done[j, 0:part] + kv
        done[j, part:2 * part] = done[j, part:2 * part] + qg

    for offset in plane:
        over_inner(done, finished, send_c, recv_c, offset).start()

    finished[inner] = done[inner]
    local_terms(SPLIT[1], SPLIT[2])
    for offset in plane:
        over_inner(mine, arrived, send_a, recv_a, offset).wait_send()
    for offset in line:
        over_outer(offset).wait_send()

    for offset in reversed(plane):
        over_inner(done, finished, send_c, recv_c, offset, True).wait_recv()

    for h in range(H):
        span = slice(h * share, (h + 1) * share)
        before[0, h] = finished[span, 0:part].reshape(E, E).astype(BF16)
        before[1, h] = finished[span, part:2 * part].reshape(E, E).astype(BF16)

    for offset in plane:
        over_inner(done, finished, send_c, recv_c, offset).wait_send()


def finish_kernel(
    n_inner, scaled, k_in, v_in, g_in, att_sum, qgrad_sum, kgrad_sum, vgrad_sum, before,
    attended, qgrad, kgrad, vgrad, att_out, qgrad_out, kgrad_out, vgrad_out, sem,
):
    rows = scaled.shape[0]
    first = (lax.axis_index("outer") * n_inner + lax.axis_index("inner")) * rows
    kv = both_heads(before[0, 0], before[0, 1])
    qg = both_heads(before[1, 0], before[1, 1])

    tiles = []
    start = 0
    for size in SIZES:
        tiles.append((start, size))
        start += size

    def store(which, source, target, tile):
        span = pl.ds(*tiles[tile])
        return pltpu.make_async_copy(source.at[span], target.at[span], sem.at[which, tile])

    stores = ((att_out, attended), (qgrad_out, qgrad), (kgrad_out, kgrad), (vgrad_out, vgrad))
    for tile, (start, size) in enumerate(tiles):
        span = pl.ds(start, size)
        att_out[span] = (att_sum[span] + dot(scaled[span], kv, NN)).astype(BF16)
        store(0, *stores[0], tile).start()
        kgrad_out[span] = (kgrad_sum[span] + dot(v_in[span], qg, NT)).astype(BF16)
        store(2, *stores[2], tile).start()
        vgrad_out[span] = (vgrad_sum[span] + dot(k_in[span], qg, NN)).astype(BF16)
        store(3, *stores[3], tile).start()
        wide = jnp.concatenate([coefficient(first + start, size)] * H, axis=1)
        qgrad_out[span] = ((qgrad_sum[span] + dot(g_in[span], kv, NT)) * wide).astype(BF16)
        store(1, *stores[1], tile).start()
    for tile in range(len(tiles)):
        for which, pair in enumerate(stores):
            store(which, *pair, tile).wait()


def on_device(n_outer, n_inner, query, keys, values, out_grad):
    rows, width = query.shape
    blocks = rows // TILE
    part = E * H // n_inner
    anywhere = pl.BlockSpec(memory_space=pl.ANY)
    in_vmem = pl.BlockSpec(memory_space=pltpu.VMEM)
    slices = pltpu.VMEM((n_inner, 2 * part, E), F32)
    dma = pltpu.SemaphoreType.DMA
    data = jax.ShapeDtypeStruct((rows, width), BF16)
    sums = jax.ShapeDtypeStruct((rows, width), F32)
    local = pl.pallas_call(
        functools.partial(local_kernel, n_outer, n_inner),
        out_shape=(data,) * 4 + (sums,) * 4 + (jax.ShapeDtypeStruct((2, H, E, E), BF16),),
        in_specs=[anywhere] * 4,
        out_specs=(in_vmem,) * 9,
        scratch_shapes=[pltpu.VMEM((blocks, H, E, E), BF16)] * 2
        + [pltpu.VMEM((2, H, E, E), F32), slices, slices, slices, pltpu.VMEM((2 * part, E), F32),
           pltpu.VMEM((n_outer, 2 * part, E), F32), slices]
        + [dma((4, rows // CHUNK)), dma((n_inner,)), dma((n_inner,)), dma((n_outer,)),
           dma((n_outer,)), dma((n_inner,)), dma((n_inner,))],
        compiler_params=pltpu.CompilerParams(
            collective_id=0, has_side_effects=True, vmem_limit_bytes=12 << 20),
        name="local",
    )(*[pltpu.with_memory_space_constraint(x, pltpu.HBM) for x in (query, keys, values, out_grad)])
    return pl.pallas_call(
        functools.partial(finish_kernel, n_inner),
        out_shape=(data,) * 4,
        in_specs=[in_vmem] * 9,
        out_specs=(anywhere,) * 4,
        scratch_shapes=[pltpu.VMEM((rows, width), BF16)] * 4 + [dma((4, len(SIZES)))],
        compiler_params=pltpu.CompilerParams(vmem_limit_bytes=16 << 20),
        name="finish",
    )(*local)


def solution(mesh):
    spec = P(("outer", "inner"), None)
    return jax.shard_map(
        functools.partial(on_device, mesh.shape["outer"], mesh.shape["inner"]),
        mesh=mesh,
        in_specs=(spec,) * 4,
        out_specs=(spec,) * 4,
        check_vma=False,
    )
```
